32 devices in a mesh: groups: 2 (over x), ctx: 16 (over z, y, core).
Axes of the slice: x: 2, y: 2, z: 4, core: 2. Of those that a mesh axis runs over, the one named last changes fastest.
Arguments:
- tokens: bfloat16 [4096, 2880], P(('groups', 'ctx')), parts along dimension 0, may hold values from -6 to 6
- lengths: int32 [8], P('groups'), parts along dimension 0, may hold values from 1 to 1536, 2048 in all
- attn_gain: float32 [2880], replicated, may hold values from 0.1 to 1.9
- w_query: bfloat16 [2880, 2048], P('ctx'), may hold values from -2 to 2
- w_key: bfloat16 [2880, 256], replicated, may hold values from -1 to 1
- w_value: bfloat16 [2880, 256], replicated, may hold values from -0.109375 to 0.109375
- sinks: float32 [32], replicated, may hold values from -2 to 4
- w_out: bfloat16 [2048, 2880], P('ctx'), may hold values from -0.5 to 0.5
- moe_gain: float32 [2880], replicated, may hold values from 0.1 to 1.9
- routes: int32 [4096, 4], P(('groups', 'ctx')), parts along dimension 0, may hold values from 0 to 7, all different within a row; in each aligned block of 128 rows (0 to 127, 128 to 255, ...) at most 68 rows name the same one
- route_weights: float32 [4096, 4], P(('groups', 'ctx')), parts along dimension 0, may hold values from 0.05 to 1
- w_gate: bfloat16 [16, 2880, 768], P('ctx'), may hold values from -0.109375 to 0.109375
- w_up: bfloat16 [16, 2880, 768], P('ctx'), may hold values from -0.109375 to 0.109375
- w_down: bfloat16 [16, 768, 2880], P('ctx'), may hold values from -0.15625 to 0.15625
Outputs:
- result: bfloat16 [4096, 2880], P(('groups', 'ctx')), parts along dimension 0
The draws below stay inside these ranges and needn't reach their ends.
There are 2 independent parts, one for each index of `groups`. The reference program is written for one: setup_inputs(seed, part) draws one part's arguments, and reference() takes and returns one part's arrays. A program takes and returns all parts, laid end to end along the dimension named above; an argument that names none is the same for every part. Nothing has to cross between parts.
Inputs may be any that keep to these rules, and one draw needn't show every extreme that they name: lengths of the 4 requests packed in order into the 2048 tokens; they sum to 2048. `routes`: each token names 4 different experts; among the 128 tokens of one index of ctx no expert is named by more than 68 tokens, a bound that some block reaches.
All inputs are finite; a program needn't handle non-finite values.
Results may differ from the reference program's by a relative error of at most 0.014.
Values may be sent and summed in bfloat16 or wider, within the bound.
A program may use at most 128 MiB of HBM per device.

```python
import math
import jax
import jax.numpy as jnp
import numpy as np
from jax import lax

D = 2880
HEADS = 32
KV = 4
HD = 64
FF = 1536
SPLITS = 2
TOP = 4
DOCS = 4
TOK_DEV = 128
SEQ = 2048
SLABS = 16
EXPERTS = 8
FF_SLAB = 768
CAP = 68
N_CTX = 16


def key_matrix(base_key):
    source = jax.random.normal(jax.random.fold_in(base_key, 11), (D, KV * HD), jnp.float32)
    return jnp.clip(source, -4.0, 4.0) / math.sqrt(D)


def draw_w_key(key, part):
    return key_matrix(key).astype(jnp.bfloat16)


def draw_w_query(key, part):
    source = jax.random.normal(jax.random.fold_in(key, 12), (D, HEADS * HD), jnp.float32)
    query_mat = jnp.clip(source, -4.0, 4.0) / math.sqrt(D)
    return query_mat.astype(jnp.bfloat16)


def steps_of(own_key, extent, pieces, least, high):
    level = 1.0
    for axis_at, blocks in pieces:
        draws = jax.random.uniform(jax.random.fold_in(jax.random.fold_in(own_key, 6), axis_at), (blocks,), jnp.float32, least / len(pieces), high / len(pieces))
        level = level * jnp.repeat(jnp.exp(draws), extent[axis_at] // blocks).reshape((-1,) + (1,) * (len(extent) - 1 - axis_at))
    return level


def length_profile(amount, total, bound, slope):
    portions = [(1 << 20) // math.isqrt(standing ** slope) + 1 for standing in range(2, amount + 1)]
    spare, holding = total - bound - (amount - 1), [1] * (amount - 1)
    while spare > 0:
        movable = [i for i in range(amount - 1) if holding[i] < bound]
        pool, left = sum([portions[i] for i in movable]), spare
        for i in movable:
            addition = min(bound - holding[i], max(1, left * portions[i] // pool), spare)
            holding[i] = holding[i] + addition
            spare = spare - addition
    return np.array([bound] + holding)


def ragged_sizes(own_key, number_of, total, bound, lean):
    if number_of == 2:
        one = jax.random.randint(own_key, (), max(1, total - bound), min(bound, total - 1) + 1)
        return jnp.stack([one, total - one])
    sizes = jnp.asarray(length_profile(number_of, total, bound, lean), jnp.int32)
    couples = (number_of - 1) // 2
    source_of, taker = sizes[1:1 + 2 * couples:2], sizes[2:2 + 2 * couples:2]
    margin = jnp.minimum(source_of - 1, bound - taker)
    moved = jax.random.randint(jax.random.fold_in(own_key, 1), (couples,), 0, 1 << 20) % (margin + 1)
    sizes = sizes.at[1:1 + 2 * couples:2].set(source_of - moved).at[2:2 + 2 * couples:2].set(taker + moved)
    return sizes[jax.random.permutation(jax.random.fold_in(own_key, 2), number_of)]


def assign_block(key, own, number, rows, number_of, top, reach, slope):
    sequence = jax.random.permutation(key, number_of)
    packed, common = portions_of(number_of, rows * top, reach, slope, True), portions_of(number_of, rows * top, reach, slope, False)
    places = jnp.arange(number_of)

    def named(sizes, turn):
        used = int((sizes > 0).sum())
        fixed = max(1, used // 4)
        shifted = fixed + (places - fixed + turn * (used - fixed)) % max(1, number_of - fixed)
        return jnp.zeros((number_of,), jnp.int32).at[sequence[jnp.where(places < fixed, places, shifted)]].set(jnp.asarray(sizes, jnp.int32))

    sizes = jnp.where(number % 4 == 0, named(packed, number // 4), named(common, number - number // 4 - 1))
    mixed = jax.random.permutation(jax.random.fold_in(own, 3), number_of)
    giver, receiver = mixed[0:number_of // 2 * 2:2], mixed[1:number_of // 2 * 2:2]
    room = jnp.minimum(sizes[giver] - 1, reach - sizes[receiver]) // 2
    room = jnp.where((giver == sequence[0]) | (receiver == sequence[0]) | (sizes[receiver] == 0), 0, jnp.maximum(room, 0))
    shifted = jax.random.randint(jax.random.fold_in(own, 4), (number_of // 2,), 0, 1 << 20) % (room + 1)
    sizes = sizes.at[giver].add(-shifted).at[receiver].add(shifted)
    labels = jnp.searchsorted(jnp.cumsum(sizes), jnp.arange(rows * top), side="right").astype(jnp.int32)
    table = labels.reshape(top, rows).T
    table = table[jax.random.permutation(jax.random.fold_in(own, 1), rows)]
    turn = jax.random.randint(jax.random.fold_in(own, 2), (rows, 1), 0, top)
    return jnp.take_along_axis(table, (jnp.arange(top)[None, :] + turn) % top, axis=1)


def portions_of(count, total, limit, skew, full):
    loads = [(1 << 20) // math.isqrt(standing ** skew) + 1 for standing in range(1, count + 1)]
    largest = limit if full else min(limit, max(-(-total // count), total * loads[0] // sum(loads)))
    least = 1 if total - largest >= count - 1 else 0
    counts, surplus = [largest] + [least] * (count - 1), total - largest - least * (count - 1)
    while surplus > 0:
        movable = [i for i in range(1, count) if counts[i] < largest] or [i for i in range(1, count) if counts[i] < limit]
        pool, left = sum([loads[i] for i in movable]), surplus
        for i in movable:
            extra = min(limit - counts[i], max(1, left * loads[i] // pool), surplus)
            counts[i] = counts[i] + extra
            surplus = surplus - extra
    return np.array(counts)


def bell_draw(own_key, shape, width, most, split=(), held_as=jnp.bfloat16):
    drawn = width * jax.random.normal(own_key, shape, jnp.float32)
    if split:
        drawn = drawn * steps_of(own_key, shape, split, -0.22, 0.18)
    return jnp.clip(drawn, -most, most).astype(held_as)


def setup_inputs(seed: int = 0, part: int = 0) -> dict:
    streams_of = jax.random.split(jax.random.key(seed), 15)
    part_keys = jax.random.split(jax.random.fold_in(streams_of[14], part), 15)
    tokens = bell_draw(part_keys[0], (SEQ, D), 1.0, 6.0, ((0, 16),))
    lengths = ragged_sizes(part_keys[1], DOCS, SEQ, 3 * SEQ // 4, 2).astype(jnp.int32)
    attn_gain = jnp.clip(1.0 + 0.18 * jax.random.normal(streams_of[2], (D,), jnp.float32), 0.1, 1.9)
    w_query = draw_w_query(jax.random.fold_in(streams_of[14], 71), part)
    w_key = draw_w_key(jax.random.fold_in(streams_of[14], 71), part)
    w_value = bell_draw(streams_of[5], (D, KV * HD), D ** -0.5, 0.109375)
    sinks = jnp.clip(jax.random.uniform(streams_of[6], (HEADS,), jnp.float32, -2.0, 4.0), -2.0, 4.0)
    w_out = bell_draw(streams_of[7], (HEADS * HD, D), (HEADS * HD // 16) ** -0.5, 0.5, ((0, 16),))
    moe_gain = jnp.clip(1.0 + 0.18 * jax.random.normal(streams_of[8], (D,), jnp.float32), 0.1, 1.9)
    routes_keys = jax.random.split(jax.random.fold_in(part_keys[9], 1), SEQ // TOK_DEV)
    routes_turns = jax.random.permutation(jax.random.fold_in(part_keys[9], 3), SEQ // TOK_DEV)
    routes = jax.vmap(lambda own, number: assign_block(jax.random.fold_in(part_keys[9], 2), own, number, TOK_DEV, EXPERTS, TOP, CAP, 1))(routes_keys, routes_turns).reshape((SEQ, TOP))
    route_weights = jnp.clip(jnp.exp(math.log(1.0) - 2.9957323 * jax.random.uniform(part_keys[10], (SEQ, TOP), jnp.float32) ** steps_of(part_keys[10], (SEQ, TOP), ((0, 16),), -0.2, 0.2)), 0.05, 1.0)
    w_gate = bell_draw(streams_of[11], (SLABS, D, FF_SLAB), D ** -0.5, 0.109375, ((0, 16),))
    w_up = bell_draw(streams_of[12], (SLABS, D, FF_SLAB), D ** -0.5, 0.109375, ((0, 16),))
    w_down = bell_draw(streams_of[13], (SLABS, FF_SLAB, D), FF ** -0.5, 0.15625, ((0, 16),))
    return dict(tokens=tokens, lengths=lengths, attn_gain=attn_gain, w_query=w_query, w_key=w_key, w_value=w_value, sinks=sinks, w_out=w_out, moe_gain=moe_gain, routes=routes, route_weights=route_weights, w_gate=w_gate, w_up=w_up, w_down=w_down)


EPS = 1e-05
THETA = 150000.0
ALPHA = 1.702
SCALE = 0.125
NEGATIVE = -1e+30

def rms_scale(values, gain_vec):
    wide = values.astype(jnp.float32)
    inverse = lax.rsqrt(lax.optimization_barrier(jnp.mean(wide * wide, axis=-1, keepdims=True)) + EPS)
    return (wide * inverse * gain_vec.astype(jnp.float32)).astype(jnp.bfloat16)

def rotate(values, positions):
    half_size = values.shape[-1] // 2
    freqs = THETA ** (-jnp.arange(half_size, dtype=jnp.float32) / half_size)
    angles = positions.astype(jnp.float32)[:, None] * freqs[None, :]
    cosine = jnp.cos(angles)[:, None, :]
    sine = jnp.sin(angles)[:, None, :]
    first = values[..., :half_size]
    second = values[..., half_size:]
    return jnp.concatenate([first * cosine - second * sine, second * cosine + first * sine], axis=-1)

def segment_of(positions, doc_ends):
    return lax.optimization_barrier(jnp.sum((positions[:, None] >= doc_ends[None, :]).astype(jnp.int32), axis=1)).astype(jnp.int32)

def expert_rows(inputs, gate_mat, up_mat, down_mat):
    gate_val = jnp.dot(inputs, gate_mat, preferred_element_type=jnp.float32)
    up_val = jnp.dot(inputs, up_mat, preferred_element_type=jnp.float32)
    hidden = ((up_val + 1.0) * gate_val * jax.nn.sigmoid(ALPHA * gate_val)).astype(jnp.bfloat16)
    return jnp.dot(hidden, down_mat, preferred_element_type=jnp.float32).astype(jnp.bfloat16)

def reference(tokens, lengths, attn_gain, w_query, w_key, w_value, sinks, w_out, moe_gain, routes, route_weights, w_gate, w_up, w_down):
    seq_len = tokens.shape[0]
    group_size = HEADS // KV
    positions = jnp.arange(seq_len, dtype=jnp.int32)
    doc_ends = jnp.cumsum(lengths).astype(jnp.int32)
    segment = segment_of(positions, doc_ends)
    normed = rms_scale(tokens, attn_gain)
    raw_query = jnp.dot(normed, w_query, preferred_element_type=jnp.float32).reshape(seq_len, HEADS, HD)
    raw_key = jnp.dot(normed, w_key, preferred_element_type=jnp.float32).reshape(seq_len, KV, HD)
    val_rot = jnp.dot(normed, w_value, preferred_element_type=jnp.float32).astype(jnp.bfloat16).reshape(seq_len, KV, HD)
    queries = rotate(raw_query, positions).astype(jnp.bfloat16)
    key_rot = rotate(raw_key, positions).astype(jnp.bfloat16)
    allowed = (segment[:, None] == segment[None, :]) & (positions[None, :] <= positions[:, None])

    def one_head(head_id):
        q_head = lax.dynamic_index_in_dim(queries, head_id, 1, keepdims=False)
        k_head = lax.dynamic_index_in_dim(key_rot, head_id // group_size, 1, keepdims=False)
        v_head = lax.dynamic_index_in_dim(val_rot, head_id // group_size, 1, keepdims=False)
        sink_val = lax.dynamic_index_in_dim(sinks, head_id, 0, keepdims=False)
        scores = jnp.dot(q_head, k_head.T, preferred_element_type=jnp.float32) * SCALE
        scores = jnp.where(allowed, scores, NEGATIVE)
        top_val = jnp.maximum(lax.optimization_barrier(jnp.max(scores, axis=1)), sink_val)
        weights = jnp.exp(scores - top_val[:, None])
        denom = lax.optimization_barrier(jnp.sum(weights, axis=1)) + jnp.exp(sink_val - top_val)
        probs = (weights / denom[:, None]).astype(jnp.bfloat16)
        return jnp.dot(probs, v_head, preferred_element_type=jnp.float32).astype(jnp.bfloat16)
    per_head = lax.map(one_head, jnp.arange(HEADS, dtype=jnp.int32))
    attended = jnp.transpose(per_head, (1, 0, 2)).reshape(seq_len, HEADS * HD)
    mixed = (tokens.astype(jnp.float32) + jnp.dot(attended, w_out, preferred_element_type=jnp.float32)).astype(jnp.bfloat16)
    expert_in = rms_scale(mixed, moe_gain)
    block_routes = routes.reshape(N_CTX, TOK_DEV * TOP)
    onehot = (block_routes[..., None] == jnp.arange(EXPERTS, dtype=jnp.int32)[None, None, :]).astype(jnp.int32)
    slots = lax.optimization_barrier(jnp.sum((jnp.cumsum(onehot, axis=1).astype(jnp.int32) - 1) * onehot, axis=2)).astype(jnp.int32)
    block_ids = jnp.arange(N_CTX, dtype=jnp.int32)[:, None]
    row_index = (block_ids * CAP + slots).reshape(-1)
    token_ids = (block_ids * TOK_DEV + jnp.arange(TOK_DEV * TOP, dtype=jnp.int32)[None, :] // TOP).reshape(-1)
    expert_ids = block_routes.reshape(-1)
    buffer = jnp.zeros((EXPERTS, N_CTX * CAP, D), jnp.bfloat16).at[expert_ids, row_index].set(expert_in[token_ids])

    def slab_out(slab_id):
        rows_in = lax.dynamic_index_in_dim(buffer, slab_id // SPLITS, 0, keepdims=False)
        return expert_rows(rows_in, w_gate[slab_id], w_up[slab_id], w_down[slab_id])
    partials = lax.map(slab_out, jnp.arange(SLABS, dtype=jnp.int32))
    summed = lax.optimization_barrier(jnp.sum(partials.reshape(EXPERTS, SPLITS, N_CTX * CAP, D).astype(jnp.float32), axis=1)).astype(jnp.bfloat16)
    summed = lax.optimization_barrier(summed).astype(jnp.float32)
    picked = summed[expert_ids, row_index].reshape(seq_len, TOP, D)
    expert_sum = lax.optimization_barrier(jnp.sum(picked * route_weights[..., None], axis=1))
    return (mixed.astype(jnp.float32) + expert_sum).astype(jnp.bfloat16)
```

```python
import functools

import jax
import jax.numpy as jnp
from jax import lax
from jax.experimental import pallas as pl
from jax.experimental.pallas import tpu as pltpu
from jax.sharding import PartitionSpec as P

HD = 64
EPS = 1e-05
THETA = 150000.0
ALPHA = 1.702
SCALE = 0.125
NEGATIVE = -1e30
MESH = pl.DeviceIdType.MESH
VMEM = pl.BlockSpec(memory_space=pltpu.VMEM)
LIMIT = 63 * 1024 * 1024


def rms_scale(values, gain_vec):
    wide = values.astype(jnp.float32)
    inverse = lax.rsqrt(jnp.mean(wide * wide, axis=-1, keepdims=True) + EPS)
    return (wide * inverse * gain_vec).astype(jnp.bfloat16)


class Ring:
    def __init__(self, chips):
        self.chips = chips
        self.me = lax.axis_index("ctx")
        self.core = lax.rem(self.me, 2)
        chip = self.me // 2
        self.fold = chips == 8
        if self.fold:
            z, y = chip // 2, lax.rem(chip, 2)
            self.pos = z + y * (chips - 1 - 2 * z)
        else:
            self.pos = chip
        self.way = 1 - 2 * self.core
        self.partner = self.me + self.way
        self.next = self.owner(-1)
        self.prev = self.owner(1)

    def index(self, pos, core):
        pos = lax.rem(pos + 2 * self.chips, self.chips)
        if self.fold:
            y = pos // (self.chips // 2)
            z = pos + y * (self.chips - 1 - 2 * pos)
            chip = z * 2 + y
        else:
            chip = pos
        return chip * 2 + core

    def owner(self, step):
        return self.index(self.pos - self.way * step, self.core)

    def partner_owner(self, step):
        return self.index(self.pos + self.way * step, 1 - self.core)

    def barrier(self):
        sem = pltpu.get_barrier_semaphore()
        for other in (self.next, self.prev, self.partner):
            pl.semaphore_signal(sem, inc=1, device_id={"ctx": other}, device_id_type=MESH)
        pl.semaphore_wait(sem, 3)


def gather_ring(ring, pieces, sems, work):
    ring_send, ring_recv, part_send, part_recv = sems
    chips = ring.chips

    def copies(i, step, own):
        source, slots, view = pieces[i]
        who = ring.owner(step)
        src = view(source) if own else view(slots.at[who])
        out = []
        for target, send, recv in (
            (ring.next, ring_send, ring_recv),
            (ring.partner, part_send, part_recv),
        ):
            at = step + 1 if target is ring.next else step
            out.append(
                pltpu.make_async_remote_copy(
                    src_ref=src,
                    dst_ref=view(slots.at[who]),
                    send_sem=send.at[i, step],
                    recv_sem=recv.at[i, at],
                    device_id={"ctx": target},
                    device_id_type=MESH,
                )
            )
        return out

    def arrived(i, step, recv, who):
        slots, view = pieces[i][1], pieces[i][2]
        ref = view(slots.at[who])
        pltpu.make_async_copy(ref, ref, recv.at[i, step]).wait()

    ring.barrier()
    for i in range(len(pieces)):
        for copy in copies(i, 0, True):
            copy.start()
    for source, slots, view in pieces:
        view(slots.at[ring.me])[...] = view(source)[...]
    work(ring.me)

    def step(s, carry):
        who = ring.owner(s)
        for i in range(len(pieces)):
            arrived(i, s, ring_recv, who)
            onward, across = copies(i, s, False)

            @pl.when(s < chips - 1)
            def _():
                onward.start()

            across.start()
        work(who)
        late = ring.partner_owner(s - 1)
        for i in range(len(pieces)):
            arrived(i, s - 1, part_recv, late)
        work(late)
        return carry

    lax.fori_loop(1, chips, step, 0)
    late = ring.partner_owner(chips - 1)
    for i in range(len(pieces)):
        arrived(i, chips - 1, part_recv, late)
    work(late)

    def drain(s, carry):
        for i in range(len(pieces)):
            onward, across = copies(i, s, False)

            @pl.when(s < chips - 1)
            def _():
                onward.wait_send()

            across.wait_send()
        return carry

    lax.fori_loop(0, chips, drain, 0)


def ring_sems(count, chips):
    return [pltpu.SemaphoreType.DMA((count, chips))] * 4


def whole(ref):
    return ref


def cols(start, size):
    return lambda ref: ref.at[:, pl.ds(start, size)]


def rows(start, size):
    return lambda ref: ref.at[pl.ds(start, size), :]


def query_kernel(chips, lhs, kv, meta, weight, out, kv_all, meta_all, slots, *sems):
    ring = Ring(chips)
    half = weight.shape[1] // 2
    pieces = [
        (kv, kv_all, whole),
        (meta, meta_all, whole),
        (weight, slots, cols(0, half)),
        (weight, slots, cols(half, half)),
    ]
    out[...] = jnp.zeros_like(out)

    def work(who):
        out[...] += jnp.dot(lhs[who], slots[who], preferred_element_type=jnp.float32)

    gather_ring(ring, pieces, sems, work)


def attend_kernel(
    chips, query, key, value, sinks, start, weight, tokens, out, slots, bias, attended, *sems
):
    ring = Ring(chips)
    blocks, tok_rows, width = attended.shape
    per_block = width // HD
    seq = key.shape[1]
    group = query.shape[0] // key.shape[0]
    half = weight.shape[0] // 2
    pieces = [(weight, slots, rows(0, half)), (weight, slots, rows(half, half))]
    key_pos = lax.broadcasted_iota(jnp.int32, (tok_rows, seq), 1)
    row_pos = lax.broadcasted_iota(jnp.int32, (tok_rows, seq), 0) + ring.me * tok_rows
    allowed = (key_pos <= row_pos) & (key_pos >= start[...])
    bias[...] = jnp.where(allowed, 0.0, NEGATIVE)

    def work(who):
        heads = []
        for j in range(per_block):
            head = who * per_block + j
            kv_head = head // group
            scores = (
                lax.dot_general(
                    query[head],
                    key[kv_head],
                    (((1,), (1,)), ((), ())),
                    preferred_element_type=jnp.float32,
                )
                + bias[...]
            )
            sink = sinks[head]
            top = jnp.maximum(jnp.max(scores, axis=1, keepdims=True), sink)
            weights = jnp.exp(scores - top)
            total = jnp.sum(weights, axis=1, keepdims=True) + jnp.exp(sink - top)
            mixed = jnp.dot(
                weights.astype(jnp.bfloat16), value[kv_head], preferred_element_type=jnp.float32
            )
            heads.append(mixed / total)
        joined = heads[0] if per_block == 1 else jnp.concatenate(heads, axis=1)
        attended[who] = joined.astype(jnp.bfloat16)

    gather_ring(ring, pieces, sems, work)
    out[...] = tokens[...].astype(jnp.float32)

    def project(d, carry):
        out[...] += jnp.dot(attended[d], slots[d], preferred_element_type=jnp.float32)
        return carry

    lax.fori_loop(0, blocks, project, 0)


def dispatch_kernel(chips, rows_in, select, out, slots, *sems):
    ring = Ring(chips)
    half = rows_in.shape[0] // 2
    pieces = [(rows_in, slots, rows(0, half)), (rows_in, slots, rows(half, half))]

    def work(who):
        out[who] = jnp.dot(select[who], slots[who], preferred_element_type=jnp.float32).astype(
            jnp.bfloat16
        )

    gather_ring(ring, pieces, sems, work)


def combine_kernel(
    chips, partial, select, weights, mixed, out, cross_out, cross_in, ring_out, ring_in,
    ring_send, ring_recv, part_send, part_recv,
):
    ring = Ring(chips)
    tok_rows = mixed.shape[0]
    half = tok_rows // 2
    ring.barrier()

    def share(who, h):
        at = pl.ds(h * half, half)
        spread = jnp.dot(select[who, at, :], partial[who], preferred_element_type=jnp.float32)
        return spread * weights[who, at, :]

    def crossing(s, h):
        at = pl.ds(h * half, half)
        return pltpu.make_async_remote_copy(
            src_ref=cross_out.at[s, at, :],
            dst_ref=cross_in.at[s, at, :],
            send_sem=part_send.at[h, s],
            recv_sem=part_recv.at[h, s],
            device_id={"ctx": ring.partner},
            device_id_type=MESH,
        )

    def onward(s, h):
        at = pl.ds(h * half, half)
        return pltpu.make_async_remote_copy(
            src_ref=ring_out.at[s, at, :],
            dst_ref=ring_in.at[s, at, :],
            send_sem=ring_send.at[h, s],
            recv_sem=ring_recv.at[h, s],
            device_id={"ctx": ring.next},
            device_id_type=MESH,
        )

    def give(s):
        who = ring.partner_owner(s + 1)
        for h in range(2):
            at = pl.ds(h * half, half)
            cross_out[s, at, :] = share(who, h).astype(jnp.bfloat16)
            crossing(s, h).start()

    def own(s, h):
        total = share(ring.owner(s + 1), h)
        crossing(s, h).wait_recv()
        return total + cross_in[s, pl.ds(h * half, half), :].astype(jnp.float32)

    give(0)
    for h in range(2):
        ring_out[0, pl.ds(h * half, half), :] = own(0, h).astype(jnp.bfloat16)
        onward(0, h).start()
    give(1)

    def step(s, carry):
        for h in range(2):
            at = pl.ds(h * half, half)
            total = own(s, h)
            onward(s - 1, h).wait_recv()
            total = total + ring_in[s - 1, at, :].astype(jnp.float32)
            ring_out[s, at, :] = total.astype(jnp.bfloat16)
            onward(s, h).start()
        give(s + 1)
        return carry

    lax.fori_loop(1, chips - 1, step, 0)
    last = chips - 1
    for h in range(2):
        at = pl.ds(h * half, half)
        total = own(last, h)
        onward(last - 1, h).wait_recv()
        total = total + ring_in[last - 1, at, :].astype(jnp.float32)
        out[at, :] = (mixed[at, :].astype(jnp.float32) + total).astype(jnp.bfloat16)

    def drain(s, carry):
        for h in range(2):
            crossing(s, h).wait_send()

            @pl.when(s < chips - 1)
            def _():
                onward(s, h).wait_send()

        return carry

    lax.fori_loop(0, chips, drain, 0)


def call(kernel, chips, out_shape, scratch, identity, *args, smem=()):
    single = not isinstance(out_shape, (list, tuple))
    return pl.pallas_call(
        functools.partial(kernel, chips),
        out_shape=out_shape,
        in_specs=[
            pl.BlockSpec(memory_space=pltpu.SMEM) if i in smem else VMEM for i in range(len(args))
        ],
        out_specs=VMEM if single else [VMEM] * len(out_shape),
        scratch_shapes=scratch,
        compiler_params=pltpu.CompilerParams(
            collective_id=identity, has_side_effects=True, vmem_limit_bytes=LIMIT
        ),
    )(*args)


def per_device(
    tokens, lengths, attn_gain, w_query, w_key, w_value, sinks, w_out, moe_gain, routes,
    route_weights, w_gate, w_up, w_down,
):
    bf16, f32 = jnp.bfloat16, jnp.float32
    tok_rows, width = tokens.shape
    devices = lax.axis_size("ctx")
    chips = devices // 2
    me = lax.axis_index("ctx")
    q_cols = w_query.shape[1]
    num_heads = q_cols // HD
    kv_cols = w_key.shape[1]
    kv_heads = kv_cols // HD
    experts = chips
    capacity = tok_rows * 4 * 17 // (16 * experts)
    padded = -(-capacity // 16) * 16

    member = routes[:, :, None] == jnp.arange(experts, dtype=jnp.int32)[None, None, :]
    named = jnp.any(member, axis=1)
    lower = jnp.tril(jnp.ones((tok_rows, tok_rows), bf16))
    slot = jnp.dot(lower, named.astype(bf16), preferred_element_type=f32) - 1.0
    slot = jnp.where(named, slot, -1.0)
    routed_weight = jnp.sum(jnp.where(member, route_weights[:, :, None], 0.0), axis=1)
    meta = jnp.concatenate([slot, routed_weight], axis=1).T

    positions = me * tok_rows + jnp.arange(tok_rows, dtype=jnp.int32)
    freqs = THETA ** (-jnp.arange(HD // 2, dtype=f32) / (HD // 2))
    angles = positions.astype(f32)[:, None] * freqs[None, :]
    cosine, sine = jnp.cos(angles)[:, None, :], jnp.sin(angles)[:, None, :]

    def rotate(values):
        first, second = values[..., : HD // 2], values[..., HD // 2 :]
        return jnp.concatenate(
            [first * cosine - second * sine, second * cosine + first * sine], axis=-1
        ).astype(bf16)

    normed = rms_scale(tokens, attn_gain)
    raw_key = jnp.dot(normed, w_key, preferred_element_type=f32)
    value = jnp.dot(normed, w_value, preferred_element_type=f32).astype(bf16)
    key = rotate(raw_key.reshape(tok_rows, kv_heads, HD)).reshape(tok_rows, kv_cols)
    kv = jnp.concatenate([key, value], axis=1)
    lhs = normed.reshape(tok_rows, devices, width // devices).transpose(1, 0, 2)
    raw_query, kv_all, meta_all = call(
        query_kernel,
        chips,
        [
            jax.ShapeDtypeStruct((tok_rows, q_cols), f32),
            jax.ShapeDtypeStruct((devices,) + kv.shape, bf16),
            jax.ShapeDtypeStruct((devices,) + meta.shape, f32),
        ],
        [pltpu.VMEM((devices,) + w_query.shape, bf16)] + ring_sems(4, chips),
        0,
        lhs, kv, meta, w_query,
    )
    query = rotate(raw_query.reshape(tok_rows, num_heads, HD)) * SCALE
    query = query.astype(bf16).transpose(1, 0, 2)
    halves = kv_all.reshape(devices * tok_rows, 2, kv_heads, HD).transpose(1, 2, 0, 3)
    doc_ends = jnp.cumsum(lengths)
    start = jnp.max(
        jnp.where(positions[:, None] >= doc_ends[None, :], doc_ends[None, :], 0), axis=1
    )[:, None]
    projected = call(
        attend_kernel,
        chips,
        jax.ShapeDtypeStruct((tok_rows, width), f32),
        [
            pltpu.VMEM((devices,) + w_out.shape, bf16),
            pltpu.VMEM((tok_rows, devices * tok_rows), f32),
            pltpu.VMEM((devices, tok_rows, w_out.shape[0]), bf16),
        ]
        + ring_sems(2, chips),
        1,
        query, halves[0], halves[1], sinks, start, w_out, tokens,
        smem=(3,),
    )
    mixed = projected.astype(bf16)
    expert_in = rms_scale(mixed, moe_gain)
    expert = me // 2
    slot_all = lax.dynamic_index_in_dim(meta_all, expert, 1, keepdims=False)
    weight_all = lax.dynamic_index_in_dim(meta_all, experts + expert, 1, keepdims=False)
    places = jnp.arange(padded, dtype=jnp.int32).astype(f32)
    select = (slot_all[:, None, :] == places[None, :, None]).astype(bf16)
    select_back = (slot_all[:, :, None] == places[None, None, :]).astype(bf16)
    packed = call(
        dispatch_kernel,
        chips,
        jax.ShapeDtypeStruct((devices, padded, width), bf16),
        [pltpu.VMEM((devices, tok_rows, width), bf16)] + ring_sems(2, chips),
        2,
        expert_in, select,
    ).reshape(devices * padded, width)
    gate_val = jnp.dot(packed, w_gate[0], preferred_element_type=f32)
    up_val = jnp.dot(packed, w_up[0], preferred_element_type=f32)
    hidden = ((up_val + 1.0) * gate_val * jax.nn.sigmoid(ALPHA * gate_val)).astype(bf16)
    partial = jnp.dot(hidden, w_down[0], preferred_element_type=f32).astype(bf16)
    return call(
        combine_kernel,
        chips,
        jax.ShapeDtypeStruct((tok_rows, width), bf16),
        [pltpu.VMEM((chips, tok_rows, width), bf16)] * 2
        + [pltpu.VMEM((chips - 1, tok_rows, width), bf16)] * 2
        + ring_sems(2, chips),
        3,
        partial.reshape(devices, padded, width), select_back, weight_all[:, :, None], mixed,
    )


def solution(mesh):
    placed = (
        P(("groups", "ctx"), None),
        P("groups"),
        P(),
        P("ctx", None),
        P(),
        P(),
        P(),
        P("ctx", None),
        P(),
        P(("groups", "ctx"), None),
        P(("groups", "ctx"), None),
        P("ctx", None, None),
        P("ctx", None, None),
        P("ctx", None, None),
    )
    return jax.shard_map(
        per_device,
        mesh=mesh,
        in_specs=placed,
        out_specs=P(("groups", "ctx"), None),
        check_vma=False,
    )
```

```python
import functools

import jax
import jax.numpy as jnp
from jax import lax
from jax.experimental import pallas as pl
from jax.experimental.pallas import tpu as pltpu
from jax.sharding import PartitionSpec as P

HD = 64
EPS = 1e-05
THETA = 150000.0
ALPHA = 1.702
SCALE = 0.125
NEGATIVE = -1e30
MESH = pl.DeviceIdType.MESH
VMEM = pl.BlockSpec(memory_space=pltpu.VMEM)
LIMIT = 63 * 1024 * 1024


def rms_scale(values, gain_vec):
    wide = values.astype(jnp.float32)
    inverse = lax.rsqrt(jnp.mean(wide * wide, axis=-1, keepdims=True) + EPS)
    return (wide * inverse * gain_vec).astype(jnp.bfloat16)


class Ring:
    def __init__(self, chips):
        self.chips = chips
        self.me = lax.axis_index("ctx")
        self.core = lax.rem(self.me, 2)
        chip = self.me // 2
        self.fold = chips == 8
        if self.fold:
            z, y = chip // 2, lax.rem(chip, 2)
            self.pos = z + y * (chips - 1 - 2 * z)
        else:
            self.pos = chip
        self.way = 1 - 2 * self.core
        self.partner = {"ctx": self.me + self.way}
        self.next = {"ctx": self.owner(-1)}
        self.prev = {"ctx": self.owner(1)}
        group = lax.axis_index("groups")
        self.parity = lax.rem(group, 2)
        self.peer = {"groups": group + 1 - 2 * self.parity}

    def index(self, pos, core):
        pos = lax.rem(pos + 2 * self.chips, self.chips)
        if self.fold:
            y = pos // (self.chips // 2)
            z = pos + y * (self.chips - 1 - 2 * pos)
            chip = z * 2 + y
        else:
            chip = pos
        return chip * 2 + core

    def owner(self, step):
        return self.index(self.pos - self.way * step, self.core)

    def partner_owner(self, step):
        return self.index(self.pos + self.way * step, 1 - self.core)

    def barrier(self, with_peer=False):
        sem = pltpu.get_barrier_semaphore()
        others = [self.next, self.prev, self.partner] + ([self.peer] if with_peer else [])
        for other in others:
            pl.semaphore_signal(sem, inc=1, device_id=other, device_id_type=MESH)
        pl.semaphore_wait(sem, len(others))


def gather_ring(ring, pieces, sems, setup, work):
    ring_send, ring_recv, part_send, part_recv, peer_send, peer_recv = sems
    chips = ring.chips
    ringed = [i for i, piece in enumerate(pieces) if piece[3] != "peer"]
    peered = [i for i, piece in enumerate(pieces) if piece[3] == "peer"]
    shared = [i for i, piece in enumerate(pieces) if piece[3] == "both"]
    lag = 2 if peered else 1

    def copy(i, step, target, send, recv, own=False):
        source, slots, view, _ = pieces[i]
        dst = view(slots.at[ring.owner(step)])
        return pltpu.make_async_remote_copy(
            src_ref=view(source) if own else dst,
            dst_ref=dst,
            send_sem=send,
            recv_sem=recv,
            device_id=target,
            device_id_type=MESH,
        )

    def onward(i, step, own=False):
        return copy(
            i, step, ring.next, ring_send.at[i, step], ring_recv.at[i, step + 1], own
        )

    def across(i, step, own=False):
        return copy(i, step, ring.partner, part_send.at[i, step], part_recv.at[i, step], own)

    def aside(i, step):
        return copy(i, step, ring.peer, peer_send.at[step], peer_recv.at[step])

    def arrived(i, sem, who):
        ref = pieces[i][2](pieces[i][1].at[who])
        pltpu.make_async_copy(ref, ref, sem).wait()

    ring.barrier(bool(peered))
    for i in ringed:
        onward(i, 0, True).start()
    for i in range(len(pieces)):
        across(i, 0, True).start()
    filled = []
    for source, slots, _, _ in pieces:
        if not any(slots is other for other in filled):
            slots[ring.me] = source[...]
            filled.append(slots)
    setup()

    def turn(t, carry):
        @pl.when(t < chips)
        def _():
            for i in ringed:
                arrived(i, ring_recv.at[i, t], ring.owner(t))

                @pl.when(t < chips - 1)
                def _():
                    onward(i, t).start()

                if i in shared:
                    aside(i, t).start()
                across(i, t).start()

        if peered:

            @pl.when((t > 1) & (t <= chips))
            def _():
                for i in peered:
                    arrived(i, peer_recv.at[t - 1], ring.owner(t - 1))
                    across(i, t - 1).start()

        @pl.when(t >= lag)
        def _():
            s = t - lag
            for i in range(len(pieces)):
                arrived(i, part_recv.at[i, s], ring.partner_owner(s))
            work(s)

        return carry

    lax.fori_loop(1, chips + lag, turn, 0)

    def drain(s, carry):
        for i in range(len(pieces)):
            across(i, s).wait_send()
        for i in ringed:

            @pl.when(s < chips - 1)
            def _():
                onward(i, s).wait_send()

        for i in shared:

            @pl.when(s > 0)
            def _():
                aside(i, s).wait_send()

        return carry

    lax.fori_loop(0, chips, drain, 0)


def ring_sems(count, chips):
    return [pltpu.SemaphoreType.DMA((count, chips))] * 4


def gather_sems(count, chips):
    return ring_sems(count, chips) + [pltpu.SemaphoreType.DMA((chips,))] * 2


def whole(ref):
    return ref


def cols(start, size):
    return lambda ref: ref.at[:, pl.ds(start, size)]


def rows(start, size):
    return lambda ref: ref.at[pl.ds(start, size), :]


def thirds(ring, source, slots):
    width = source.shape[1]
    third = width // 3 // 128 * 128
    mine = pl.multiple_of(ring.parity * third, 128)
    other = pl.multiple_of((1 - ring.parity) * third, 128)
    return [
        (source, slots, cols(mine, third), "both"),
        (source, slots, cols(2 * third, width - 2 * third), "ring"),
        (source, slots, cols(other, third), "peer"),
    ]


def query_kernel(chips, lhs, kv, meta, weight, out, kv_all, meta_all, slots, *sems):
    ring = Ring(chips)
    pieces = [(kv, kv_all, whole, "ring"), (meta, meta_all, whole, "ring")]
    pieces += thirds(ring, weight, slots)

    def setup():
        out[...] = jnp.zeros_like(out)

    def work(s):
        for who in (ring.owner(s), ring.partner_owner(s)):
            out[...] += jnp.dot(lhs[who], slots[who], preferred_element_type=jnp.float32)

    gather_ring(ring, pieces, sems, setup, work)


def attend_kernel(
    chips, raw, kv_all, cosine, sine, sinks, start, weight, tokens,
    out, slots, bias, query, key, value, attended, *sems
):
    ring = Ring(chips)
    blocks, tok_rows, width = attended.shape
    per_block = width // HD
    kv_heads, seq, _ = key.shape
    group = query.shape[0] // kv_heads
    pieces = thirds(ring, weight, slots)

    def setup():
        key_pos = lax.broadcasted_iota(jnp.int32, (tok_rows, seq), 1)
        row_pos = lax.broadcasted_iota(jnp.int32, (tok_rows, seq), 0) + ring.me * tok_rows
        allowed = (key_pos <= row_pos) & (key_pos >= start[...])
        bias[...] = jnp.where(allowed, 0.0, NEGATIVE)
        lane = lax.broadcasted_iota(jnp.int32, (tok_rows, 2 * HD), 1)
        first = lax.rem(lane, HD) < HD // 2

        def turn_pair(j, carry):
            pair = raw[:, pl.ds(pl.multiple_of(j * 2 * HD, 2 * HD), 2 * HD)]
            other = jnp.where(
                first, pltpu.roll(pair, 2 * HD - HD // 2, 1), pltpu.roll(pair, HD // 2, 1)
            )
            turned = ((pair * cosine[...] + other * sine[...]) * SCALE).astype(jnp.bfloat16)
            query[2 * j] = turned[:, :HD]
            query[2 * j + 1] = turned[:, HD:]
            return carry

        lax.fori_loop(0, query.shape[0] // 2, turn_pair, 0)

        def unpack(d, carry):
            at = pl.ds(pl.multiple_of(d * tok_rows, tok_rows), tok_rows)
            block = kv_all[d]
            for g in range(kv_heads):
                key[g, at, :] = block[:, g * HD : (g + 1) * HD]
                value[g, at, :] = block[:, (kv_heads + g) * HD : (kv_heads + g + 1) * HD]
            return carry

        lax.fori_loop(0, blocks, unpack, 0)

    def attend(who):
        heads = []
        for j in range(per_block):
            head = who * per_block + j
            kv_head = head // group
            scores = (
                lax.dot_general(
                    query[head],
                    key[kv_head],
                    (((1,), (1,)), ((), ())),
                    preferred_element_type=jnp.float32,
                )
                + bias[...]
            )
            sink = sinks[head]
            top = jnp.maximum(jnp.max(scores, axis=1, keepdims=True), sink)
            weights = jnp.exp(scores - top)
            total = jnp.sum(weights, axis=1, keepdims=True) + jnp.exp(sink - top)
            mixed = jnp.dot(
                weights.astype(jnp.bfloat16), value[kv_head], preferred_element_type=jnp.float32
            )
            heads.append(mixed / total)
        joined = heads[0] if per_block == 1 else jnp.concatenate(heads, axis=1)
        attended[who] = joined.astype(jnp.bfloat16)

    def work(s):
        attend(ring.owner(s))
        attend(ring.partner_owner(s))

    gather_ring(ring, pieces, sems, setup, work)
    out[...] = tokens[...].astype(jnp.float32)

    def project(d, carry):
        out[...] += jnp.dot(attended[d], slots[d], preferred_element_type=jnp.float32)
        return carry

    lax.fori_loop(0, blocks, project, 0)


def expert_kernel(
    chips, rows_in, select, w_gate, w_up, w_down,
    out, slots, packed, gate, up, down, load_sem, *sems
):
    ring = Ring(chips)
    half = rows_in.shape[0] // 2
    padded = select.shape[1]
    pieces = [
        (rows_in, slots, rows(0, half), "ring"),
        (rows_in, slots, rows(half, half), "ring"),
    ]
    loads = [
        pltpu.make_async_copy(source, target, load_sem.at[i])
        for i, (source, target) in enumerate(((w_gate, gate), (w_up, up), (w_down, down)))
    ]
    for load in loads:
        load.start()

    def work(s):
        whose = [
            ring.owner(s - 1), ring.partner_owner(s - 1), ring.owner(s), ring.partner_owner(s)
        ]

        @pl.when(s == 1)
        def _():
            for load in loads:
                load.wait()

        @pl.when(lax.rem(s, 2) == 1)
        def _():
            for j, who in enumerate(whose):
                packed[j * padded : (j + 1) * padded, :] = jnp.dot(
                    select[who], slots[who], preferred_element_type=jnp.float32
                ).astype(jnp.bfloat16)
            gate_val = jnp.dot(packed[...], gate[...], preferred_element_type=jnp.float32)
            up_val = jnp.dot(packed[...], up[...], preferred_element_type=jnp.float32)
            hidden = (up_val + 1.0) * gate_val * jax.nn.sigmoid(ALPHA * gate_val)
            partial = jnp.dot(
                hidden.astype(jnp.bfloat16), down[...], preferred_element_type=jnp.float32
            ).astype(jnp.bfloat16)
            for j, who in enumerate(whose):
                out[who] = partial[j * padded : (j + 1) * padded, :]

    gather_ring(ring, pieces, sems, lambda: None, work)


def combine_kernel(
    chips, partial, select, weights, mixed, out, cross_out, cross_in, ring_out, ring_in,
    ring_send, ring_recv, part_send, part_recv,
):
    ring = Ring(chips)
    tok_rows = mixed.shape[0]
    half = tok_rows // 2
    ring.barrier()

    def share(who, h):
        at = pl.ds(h * half, half)
        spread = jnp.dot(select[who, at, :], partial[who], preferred_element_type=jnp.float32)
        return spread * weights[who, at, :]

    def crossing(s, h):
        at = pl.ds(h * half, half)
        return pltpu.make_async_remote_copy(
            src_ref=cross_out.at[s, at, :],
            dst_ref=cross_in.at[s, at, :],
            send_sem=part_send.at[h, s],
            recv_sem=part_recv.at[h, s],
            device_id=ring.partner,
            device_id_type=MESH,
        )

    def onward(s, h):
        at = pl.ds(h * half, half)
        return pltpu.make_async_remote_copy(
            src_ref=ring_out.at[s, at, :],
            dst_ref=ring_in.at[s, at, :],
            send_sem=ring_send.at[h, s],
            recv_sem=ring_recv.at[h, s],
            device_id=ring.next,
            device_id_type=MESH,
        )

    def give(s):
        who = ring.partner_owner(s + 1)
        for h in range(2):
            at = pl.ds(h * half, half)
            cross_out[s, at, :] = share(who, h).astype(jnp.bfloat16)
            crossing(s, h).start()

    def own(s, h):
        total = share(ring.owner(s + 1), h)
        crossing(s, h).wait_recv()
        return total + cross_in[s, pl.ds(h * half, half), :].astype(jnp.float32)

    give(0)
    for h in range(2):
        ring_out[0, pl.ds(h * half, half), :] = own(0, h).astype(jnp.bfloat16)
        onward(0, h).start()
    give(1)

    def step(s, carry):
        for h in range(2):
            at = pl.ds(h * half, half)
            total = own(s, h)
            onward(s - 1, h).wait_recv()
            total = total + ring_in[s - 1, at, :].astype(jnp.float32)
            ring_out[s, at, :] = total.astype(jnp.bfloat16)
            onward(s, h).start()
        give(s + 1)
        return carry

    lax.fori_loop(1, chips - 1, step, 0)
    last = chips - 1
    for h in range(2):
        at = pl.ds(h * half, half)
        total = own(last, h)
        onward(last - 1, h).wait_recv()
        total = total + ring_in[last - 1, at, :].astype(jnp.float32)
        out[at, :] = (mixed[at, :].astype(jnp.float32) + total).astype(jnp.bfloat16)

    def drain(s, carry):
        for h in range(2):
            crossing(s, h).wait_send()

            @pl.when(s < chips - 1)
            def _():
                onward(s, h).wait_send()

        return carry

    lax.fori_loop(0, chips, drain, 0)


def call(kernel, chips, out_shape, scratch, identity, *args, smem=(), hbm=()):
    single = not isinstance(out_shape, (list, tuple))
    return pl.pallas_call(
        functools.partial(kernel, chips),
        out_shape=out_shape,
        in_specs=[
            pl.BlockSpec(memory_space=pltpu.SMEM)
            if i in smem
            else pl.BlockSpec(memory_space=pl.ANY)
            if i in hbm
            else VMEM
            for i in range(len(args))
        ],
        out_specs=VMEM if single else [VMEM] * len(out_shape),
        scratch_shapes=scratch,
        compiler_params=pltpu.CompilerParams(
            collective_id=identity, has_side_effects=True, vmem_limit_bytes=LIMIT
        ),
    )(*args)


def per_device(
    tokens, lengths, attn_gain, w_query, w_key, w_value, sinks, w_out, moe_gain, routes,
    route_weights, w_gate, w_up, w_down,
):
    bf16, f32 = jnp.bfloat16, jnp.float32
    tok_rows, width = tokens.shape
    devices = lax.axis_size("ctx")
    chips = devices // 2
    me = lax.axis_index("ctx")
    q_cols = w_query.shape[1]
    num_heads = q_cols // HD
    kv_cols = w_key.shape[1]
    kv_heads = kv_cols // HD
    experts = chips
    capacity = tok_rows * 4 * 17 // (16 * experts)
    padded = -(-capacity // 16) * 16

    member = routes[:, :, None] == jnp.arange(experts, dtype=jnp.int32)[None, None, :]
    named = jnp.any(member, axis=1)
    lower = jnp.tril(jnp.ones((tok_rows, tok_rows), bf16))
    slot = jnp.dot(lower, named.astype(bf16), preferred_element_type=f32) - 1.0
    slot = jnp.where(named, slot, -1.0)
    routed_weight = jnp.sum(jnp.where(member, route_weights[:, :, None], 0.0), axis=1)
    meta = jnp.concatenate([slot, routed_weight], axis=1).T

    positions = me * tok_rows + jnp.arange(tok_rows, dtype=jnp.int32)
    freqs = THETA ** (-jnp.arange(HD // 2, dtype=f32) / (HD // 2))
    angles = positions.astype(f32)[:, None] * freqs[None, :]
    cosine, sine = jnp.cos(angles)[:, None, :], jnp.sin(angles)[:, None, :]

    def rotate(values):
        first, second = values[..., : HD // 2], values[..., HD // 2 :]
        return jnp.concatenate(
            [first * cosine - second * sine, second * cosine + first * sine], axis=-1
        ).astype(bf16)

    normed = rms_scale(tokens, attn_gain)
    raw_key = jnp.dot(normed, w_key, preferred_element_type=f32)
    value = jnp.dot(normed, w_value, preferred_element_type=f32).astype(bf16)
    key = rotate(raw_key.reshape(tok_rows, kv_heads, HD)).reshape(tok_rows, kv_cols)
    kv = jnp.concatenate([key, value], axis=1)
    lhs = normed.reshape(tok_rows, devices, width // devices).transpose(1, 0, 2)
    raw_query, kv_all, meta_all = call(
        query_kernel,
        chips,
        [
            jax.ShapeDtypeStruct((tok_rows, q_cols), f32),
            jax.ShapeDtypeStruct((devices,) + kv.shape, bf16),
            jax.ShapeDtypeStruct((devices,) + meta.shape, f32),
        ],
        [pltpu.VMEM((devices,) + w_query.shape, bf16)] + gather_sems(5, chips),
        0,
        lhs, kv, meta, w_query,
    )
    cosine_pair = jnp.tile(cosine[:, 0, :], (1, 4))
    sine_pair = jnp.tile(jnp.concatenate([-sine[:, 0, :], sine[:, 0, :]], axis=1), (1, 2))
    doc_ends = jnp.cumsum(lengths)
    start = jnp.max(
        jnp.where(positions[:, None] >= doc_ends[None, :], doc_ends[None, :], 0), axis=1
    )[:, None]
    projected = call(
        attend_kernel,
        chips,
        jax.ShapeDtypeStruct((tok_rows, width), f32),
        [
            pltpu.VMEM((devices,) + w_out.shape, bf16),
            pltpu.VMEM((tok_rows, devices * tok_rows), f32),
            pltpu.VMEM((num_heads, tok_rows, HD), bf16),
            pltpu.VMEM((kv_heads, devices * tok_rows, HD), bf16),
            pltpu.VMEM((kv_heads, devices * tok_rows, HD), bf16),
            pltpu.VMEM((devices, tok_rows, w_out.shape[0]), bf16),
        ]
        + gather_sems(3, chips),
        1,
        raw_query, kv_all, cosine_pair, sine_pair, sinks, start, w_out, tokens,
        smem=(4,),
    )
    mixed = projected.astype(bf16)
    expert_in = rms_scale(mixed, moe_gain)
    expert = me // 2
    slot_all = lax.dynamic_index_in_dim(meta_all, expert, 1, keepdims=False)
    weight_all = lax.dynamic_index_in_dim(meta_all, experts + expert, 1, keepdims=False)
    places = jnp.arange(padded, dtype=jnp.int32).astype(f32)
    select = (slot_all[:, None, :] == places[None, :, None]).astype(bf16)
    select_back = (slot_all[:, :, None] == places[None, None, :]).astype(bf16)
    partial = call(
        expert_kernel,
        chips,
        jax.ShapeDtypeStruct((devices, padded, width), bf16),
        [
            pltpu.VMEM((devices, tok_rows, width), bf16),
            pltpu.VMEM((4 * padded, width), bf16),
            pltpu.VMEM(w_gate.shape[1:], bf16),
            pltpu.VMEM(w_up.shape[1:], bf16),
            pltpu.VMEM(w_down.shape[1:], bf16),
            pltpu.SemaphoreType.DMA((3,)),
        ]
        + gather_sems(2, chips),
        2,
        expert_in, select, w_gate[0], w_up[0], w_down[0],
        hbm=(2, 3, 4),
    )
    return call(
        combine_kernel,
        chips,
        jax.ShapeDtypeStruct((tok_rows, width), bf16),
        [pltpu.VMEM((chips, tok_rows, width), bf16)] * 2
        + [pltpu.VMEM((chips - 1, tok_rows, width), bf16)] * 2
        + ring_sems(2, chips),
        3,
        partial, select_back, weight_all[:, :, None], mixed,
    )


def solution(mesh):
    placed = (
        P(("groups", "ctx"), None),
        P("groups"),
        P(),
        P("ctx", None),
        P(),
        P(),
        P(),
        P("ctx", None),
        P(),
        P(("groups", "ctx"), None),
        P(("groups", "ctx"), None),
        P("ctx", None, None),
        P("ctx", None, None),
        P("ctx", None, None),
    )
    return jax.shard_map(
        per_device,
        mesh=mesh,
        in_specs=placed,
        out_specs=P(("groups", "ctx"), None),
        check_vma=False,
    )
```

```python
import functools

import jax
import jax.numpy as jnp
from jax import lax
from jax.experimental import pallas as pl
from jax.experimental.pallas import tpu as pltpu
from jax.sharding import PartitionSpec as P

HD = 64
EPS = 1e-05
THETA = 150000.0
ALPHA = 1.702
SCALE = 0.125
NEGATIVE = -1e30
MESH = pl.DeviceIdType.MESH
VMEM = pl.BlockSpec(memory_space=pltpu.VMEM)
LIMIT = 63 * 1024 * 1024


def rms_scale(values, gain_vec):
    wide = values.astype(jnp.float32)
    inverse = lax.rsqrt(jnp.mean(wide * wide, axis=-1, keepdims=True) + EPS)
    return (wide * inverse * gain_vec).astype(jnp.bfloat16)


class Ring:
    def __init__(self, chips):
        self.chips = chips
        self.me = lax.axis_index("ctx")
        self.core = lax.rem(self.me, 2)
        chip = self.me // 2
        self.fold = chips == 8
        if self.fold:
            z, y = chip // 2, lax.rem(chip, 2)
            self.pos = z + y * (chips - 1 - 2 * z)
        else:
            self.pos = chip
        self.way = 1 - 2 * self.core
        self.partner = {"ctx": self.me + self.way}
        self.next = {"ctx": self.owner(-1)}
        self.prev = {"ctx": self.owner(1)}
        group = lax.axis_index("groups")
        self.parity = lax.rem(group, 2)
        self.peer = {"groups": group + 1 - 2 * self.parity}

    def index(self, pos, core):
        pos = lax.rem(pos + 2 * self.chips, self.chips)
        if self.fold:
            y = pos // (self.chips // 2)
            z = pos + y * (self.chips - 1 - 2 * pos)
            chip = z * 2 + y
        else:
            chip = pos
        return chip * 2 + core

    def owner(self, step):
        return self.index(self.pos - self.way * step, self.core)

    def partner_owner(self, step):
        return self.index(self.pos + self.way * step, 1 - self.core)

    def barrier(self, with_peer=False):
        sem = pltpu.get_barrier_semaphore()
        others = [self.next, self.prev, self.partner] + ([self.peer] if with_peer else [])
        for other in others:
            pl.semaphore_signal(sem, inc=1, device_id=other, device_id_type=MESH)
        pl.semaphore_wait(sem, len(others))


def gather_ring(ring, pieces, sems, setup, work):
    ring_send, ring_recv, part_send, part_recv, peer_send, peer_recv = sems
    chips = ring.chips
    ringed = [i for i, piece in enumerate(pieces) if piece[3] != "peer"]
    peered = [i for i, piece in enumerate(pieces) if piece[3] == "peer"]
    shared = [i for i, piece in enumerate(pieces) if piece[3] == "both"]
    lag = 2 if peered else 1

    def copy(i, step, target, send, recv, own=False):
        source, slots, view, _ = pieces[i]
        dst = view(slots.at[ring.owner(step)])
        return pltpu.make_async_remote_copy(
            src_ref=view(source) if own else dst,
            dst_ref=dst,
            send_sem=send,
            recv_sem=recv,
            device_id=target,
            device_id_type=MESH,
        )

    def onward(i, step, own=False):
        return copy(
            i, step, ring.next, ring_send.at[i, step], ring_recv.at[i, step + 1], own
        )

    def across(i, step, own=False):
        return copy(i, step, ring.partner, part_send.at[i, step], part_recv.at[i, step], own)

    def aside(i, step):
        return copy(i, step, ring.peer, peer_send.at[step], peer_recv.at[step])

    def arrived(i, sem, who):
        ref = pieces[i][2](pieces[i][1].at[who])
        pltpu.make_async_copy(ref, ref, sem).wait()

    ring.barrier(bool(peered))
    for i in ringed:
        onward(i, 0, True).start()
    for i in range(len(pieces)):
        across(i, 0, True).start()
    filled = []
    for source, slots, _, _ in pieces:
        if not any(slots is other for other in filled):
            slots[ring.me] = source[...]
            filled.append(slots)
    setup()

    def turn(t, carry):
        @pl.when(t < chips)
        def _():
            for i in ringed:
                arrived(i, ring_recv.at[i, t], ring.owner(t))

                @pl.when(t < chips - 1)
                def _():
                    onward(i, t).start()

                if i in shared:
                    aside(i, t).start()
                across(i, t).start()

        if peered:

            @pl.when((t > 1) & (t <= chips))
            def _():
                for i in peered:
                    arrived(i, peer_recv.at[t - 1], ring.owner(t - 1))
                    across(i, t - 1).start()

        @pl.when(t >= lag)
        def _():
            s = t - lag
            for i in range(len(pieces)):
                arrived(i, part_recv.at[i, s], ring.partner_owner(s))
            work(s)

        return carry

    lax.fori_loop(1, chips + lag, turn, 0)

    def drain(s, carry):
        for i in range(len(pieces)):
            across(i, s).wait_send()
        for i in ringed:

            @pl.when(s < chips - 1)
            def _():
                onward(i, s).wait_send()

        for i in shared:

            @pl.when(s > 0)
            def _():
                aside(i, s).wait_send()

        return carry

    lax.fori_loop(0, chips, drain, 0)


def ring_sems(count, chips):
    return [pltpu.SemaphoreType.DMA((count, chips))] * 4


def gather_sems(count, chips):
    return ring_sems(count, chips) + [pltpu.SemaphoreType.DMA((chips,))] * 2


def whole(ref):
    return ref


def cols(start, size):
    return lambda ref: ref.at[:, pl.ds(start, size)]


def rows(start, size):
    return lambda ref: ref.at[pl.ds(start, size), :]


def thirds(ring, source, slots):
    width = source.shape[1]
    third = width // 3 // 128 * 128
    mine = pl.multiple_of(ring.parity * third, 128)
    other = pl.multiple_of((1 - ring.parity) * third, 128)
    return [
        (source, slots, cols(mine, third), "both"),
        (source, slots, cols(2 * third, width - 2 * third), "ring"),
        (source, slots, cols(other, third), "peer"),
    ]


def query_kernel(chips, lhs, kv, meta, weight, out, kv_all, meta_all, slots, *sems):
    ring = Ring(chips)
    pieces = [(kv, kv_all, whole, "ring"), (meta, meta_all, whole, "ring")]
    pieces += thirds(ring, weight, slots)

    def setup():
        out[...] = jnp.zeros_like(out)

    def work(s):
        for who in (ring.owner(s), ring.partner_owner(s)):
            out[...] += jnp.dot(lhs[who], slots[who], preferred_element_type=jnp.float32)

    gather_ring(ring, pieces, sems, setup, work)


def attend_kernel(
    chips, raw, kv_all, cosine, sine, sinks, start, weight, tokens, gain,
    mixed_out, expert_in, out, slots, bias, query, key, value, attended, *sems
):
    ring = Ring(chips)
    blocks, tok_rows, width = attended.shape
    per_block = width // HD
    kv_heads, seq, _ = key.shape
    group = query.shape[0] // kv_heads
    pieces = thirds(ring, weight, slots)

    def setup():
        key_pos = lax.broadcasted_iota(jnp.int32, (tok_rows, seq), 1)
        row_pos = lax.broadcasted_iota(jnp.int32, (tok_rows, seq), 0) + ring.me * tok_rows
        allowed = (key_pos <= row_pos) & (key_pos >= start[...])
        bias[...] = jnp.where(allowed, 0.0, NEGATIVE)
        lane = lax.broadcasted_iota(jnp.int32, (tok_rows, 2 * HD), 1)
        first = lax.rem(lane, HD) < HD // 2

        def turn_pair(j, carry):
            pair = raw[:, pl.ds(pl.multiple_of(j * 2 * HD, 2 * HD), 2 * HD)]
            other = jnp.where(
                first, pltpu.roll(pair, 2 * HD - HD // 2, 1), pltpu.roll(pair, HD // 2, 1)
            )
            turned = ((pair * cosine[...] + other * sine[...]) * SCALE).astype(jnp.bfloat16)
            query[2 * j] = turned[:, :HD]
            query[2 * j + 1] = turned[:, HD:]
            return carry

        lax.fori_loop(0, query.shape[0] // 2, turn_pair, 0)

        def unpack(d, carry):
            at = pl.ds(pl.multiple_of(d * tok_rows, tok_rows), tok_rows)
            block = kv_all[d]
            for g in range(kv_heads):
                key[g, at, :] = block[:, g * HD : (g + 1) * HD]
                value[g, at, :] = block[:, (kv_heads + g) * HD : (kv_heads + g + 1) * HD]
            return carry

        lax.fori_loop(0, blocks, unpack, 0)

    def attend(who):
        heads = []
        for j in range(per_block):
            head = who * per_block + j
            kv_head = head // group
            scores = (
                lax.dot_general(
                    query[head],
                    key[kv_head],
                    (((1,), (1,)), ((), ())),
                    preferred_element_type=jnp.float32,
                )
                + bias[...]
            )
            sink = sinks[head]
            top = jnp.maximum(jnp.max(scores, axis=1, keepdims=True), sink)
            weights = jnp.exp(scores - top)
            total = jnp.sum(weights, axis=1, keepdims=True) + jnp.exp(sink - top)
            mixed = jnp.dot(
                weights.astype(jnp.bfloat16), value[kv_head], preferred_element_type=jnp.float32
            )
            heads.append(mixed / total)
        joined = heads[0] if per_block == 1 else jnp.concatenate(heads, axis=1)
        attended[who] = joined.astype(jnp.bfloat16)

    def work(s):
        attend(ring.owner(s))
        attend(ring.partner_owner(s))

    gather_ring(ring, pieces, sems, setup, work)
    out[...] = tokens[...].astype(jnp.float32)

    def project(d, carry):
        out[...] += jnp.dot(attended[d], slots[d], preferred_element_type=jnp.float32)
        return carry

    lax.fori_loop(0, blocks, project, 0)
    mixed_out[...] = out[...].astype(jnp.bfloat16)
    expert_in[...] = rms_scale(mixed_out[...], gain[...])


def expert_kernel(
    chips, rows_in, select, w_gate, w_up, w_down,
    out, slots, packed, gate, up, down, load_sem, *sems
):
    ring = Ring(chips)
    half = rows_in.shape[0] // 2
    padded = select.shape[1]
    pieces = [
        (rows_in, slots, rows(0, half), "ring"),
        (rows_in, slots, rows(half, half), "ring"),
    ]
    loads = [
        pltpu.make_async_copy(source, target, load_sem.at[i])
        for i, (source, target) in enumerate(((w_gate, gate), (w_up, up), (w_down, down)))
    ]
    for load in loads:
        load.start()

    def work(s):
        whose = [
            ring.owner(s - 1), ring.partner_owner(s - 1), ring.owner(s), ring.partner_owner(s)
        ]

        @pl.when(s == 1)
        def _():
            for load in loads:
                load.wait()

        @pl.when(lax.rem(s, 2) == 1)
        def _():
            for j, who in enumerate(whose):
                packed[j * padded : (j + 1) * padded, :] = jnp.dot(
                    select[who], slots[who], preferred_element_type=jnp.float32
                ).astype(jnp.bfloat16)
            gate_val = jnp.dot(packed[...], gate[...], preferred_element_type=jnp.float32)
            up_val = jnp.dot(packed[...], up[...], preferred_element_type=jnp.float32)
            hidden = (up_val + 1.0) * gate_val * jax.nn.sigmoid(ALPHA * gate_val)
            partial = lax.dot_general(
                hidden.astype(jnp.bfloat16),
                down[...],
                (((1,), (1,)), ((), ())),
                preferred_element_type=jnp.float32,
            ).astype(jnp.bfloat16)
            for j, who in enumerate(whose):
                out[who] = partial[j * padded : (j + 1) * padded, :]

    gather_ring(ring, pieces, sems, lambda: None, work)


def combine_kernel(
    chips, partial, select, weights, mixed, out, cross_out, cross_in, ring_out, ring_in,
    ring_send, ring_recv, part_send, part_recv,
):
    ring = Ring(chips)
    tok_rows = mixed.shape[0]
    half = tok_rows // 2
    ring.barrier()

    def share(who, h):
        at = pl.ds(h * half, half)
        spread = jnp.dot(select[who, at, :], partial[who], preferred_element_type=jnp.float32)
        return spread * weights[who, at, :]

    def crossing(s, h):
        at = pl.ds(h * half, half)
        return pltpu.make_async_remote_copy(
            src_ref=cross_out.at[s, at, :],
            dst_ref=cross_in.at[s, at, :],
            send_sem=part_send.at[h, s],
            recv_sem=part_recv.at[h, s],
            device_id=ring.partner,
            device_id_type=MESH,
        )

    def onward(s, h):
        at = pl.ds(h * half, half)
        return pltpu.make_async_remote_copy(
            src_ref=ring_out.at[s, at, :],
            dst_ref=ring_in.at[s, at, :],
            send_sem=ring_send.at[h, s],
            recv_sem=ring_recv.at[h, s],
            device_id=ring.next,
            device_id_type=MESH,
        )

    def give(s):
        who = ring.partner_owner(s + 1)
        for h in range(2):
            at = pl.ds(h * half, half)
            cross_out[s, at, :] = share(who, h).astype(jnp.bfloat16)
            crossing(s, h).start()

    def own(s, h):
        total = share(ring.owner(s + 1), h)
        crossing(s, h).wait_recv()
        return total + cross_in[s, pl.ds(h * half, half), :].astype(jnp.float32)

    give(0)
    for h in range(2):
        ring_out[0, pl.ds(h * half, half), :] = own(0, h).astype(jnp.bfloat16)
        onward(0, h).start()
    give(1)

    def step(s, carry):
        for h in range(2):
            at = pl.ds(h * half, half)
            total = own(s, h)
            onward(s - 1, h).wait_recv()
            total = total + ring_in[s - 1, at, :].astype(jnp.float32)
            ring_out[s, at, :] = total.astype(jnp.bfloat16)
            onward(s, h).start()
        give(s + 1)
        return carry

    lax.fori_loop(1, chips - 1, step, 0)
    last = chips - 1
    for h in range(2):
        at = pl.ds(h * half, half)
        total = own(last, h)
        onward(last - 1, h).wait_recv()
        total = total + ring_in[last - 1, at, :].astype(jnp.float32)
        out[at, :] = (mixed[at, :].astype(jnp.float32) + total).astype(jnp.bfloat16)

    def drain(s, carry):
        for h in range(2):
            crossing(s, h).wait_send()

            @pl.when(s < chips - 1)
            def _():
                onward(s, h).wait_send()

        return carry

    lax.fori_loop(0, chips, drain, 0)


def call(kernel, chips, out_shape, scratch, identity, *args, smem=(), hbm=()):
    single = not isinstance(out_shape, (list, tuple))
    return pl.pallas_call(
        functools.partial(kernel, chips),
        out_shape=out_shape,
        in_specs=[
            pl.BlockSpec(memory_space=pltpu.SMEM)
            if i in smem
            else pl.BlockSpec(memory_space=pl.ANY)
            if i in hbm
            else VMEM
            for i in range(len(args))
        ],
        out_specs=VMEM if single else [VMEM] * len(out_shape),
        scratch_shapes=scratch,
        compiler_params=pltpu.CompilerParams(
            collective_id=identity, has_side_effects=True, vmem_limit_bytes=LIMIT
        ),
    )(*args)


def per_device(
    tokens, lengths, attn_gain, w_query, w_key, w_value, sinks, w_out, moe_gain, routes,
    route_weights, w_gate, w_up, w_down,
):
    bf16, f32 = jnp.bfloat16, jnp.float32
    tok_rows, width = tokens.shape
    devices = lax.axis_size("ctx")
    chips = devices // 2
    me = lax.axis_index("ctx")
    q_cols = w_query.shape[1]
    num_heads = q_cols // HD
    kv_cols = w_key.shape[1]
    kv_heads = kv_cols // HD
    experts = chips
    capacity = tok_rows * 4 * 17 // (16 * experts)
    padded = -(-capacity // 16) * 16

    member = routes[:, :, None] == jnp.arange(experts, dtype=jnp.int32)[None, None, :]
    named = jnp.any(member, axis=1)
    lower = jnp.tril(jnp.ones((tok_rows, tok_rows), bf16))
    slot = jnp.dot(lower, named.astype(bf16), preferred_element_type=f32) - 1.0
    slot = jnp.where(named, slot, -1.0)
    routed_weight = jnp.sum(jnp.where(member, route_weights[:, :, None], 0.0), axis=1)
    meta = jnp.concatenate([slot, routed_weight], axis=1).T

    positions = me * tok_rows + jnp.arange(tok_rows, dtype=jnp.int32)
    freqs = THETA ** (-jnp.arange(HD // 2, dtype=f32) / (HD // 2))
    angles = positions.astype(f32)[:, None] * freqs[None, :]
    cosine, sine = jnp.cos(angles)[:, None, :], jnp.sin(angles)[:, None, :]

    def rotate(values):
        first, second = values[..., : HD // 2], values[..., HD // 2 :]
        return jnp.concatenate(
            [first * cosine - second * sine, second * cosine + first * sine], axis=-1
        ).astype(bf16)

    normed = rms_scale(tokens, attn_gain)
    raw_key = jnp.dot(normed, w_key, preferred_element_type=f32)
    value = jnp.dot(normed, w_value, preferred_element_type=f32).astype(bf16)
    key = rotate(raw_key.reshape(tok_rows, kv_heads, HD)).reshape(tok_rows, kv_cols)
    kv = jnp.concatenate([key, value], axis=1)
    lhs = normed.reshape(tok_rows, devices, width // devices).transpose(1, 0, 2)
    raw_query, kv_all, meta_all = call(
        query_kernel,
        chips,
        [
            jax.ShapeDtypeStruct((tok_rows, q_cols), f32),
            jax.ShapeDtypeStruct((devices,) + kv.shape, bf16),
            jax.ShapeDtypeStruct((devices,) + meta.shape, f32),
        ],
        [pltpu.VMEM((devices,) + w_query.shape, bf16)] + gather_sems(5, chips),
        0,
        lhs, kv, meta, w_query,
    )
    cosine_pair = jnp.tile(cosine[:, 0, :], (1, 4))
    sine_pair = jnp.tile(jnp.concatenate([-sine[:, 0, :], sine[:, 0, :]], axis=1), (1, 2))
    doc_ends = jnp.cumsum(lengths)
    start = jnp.max(
        jnp.where(positions[:, None] >= doc_ends[None, :], doc_ends[None, :], 0), axis=1
    )[:, None]
    mixed, expert_in = call(
        attend_kernel,
        chips,
        [jax.ShapeDtypeStruct((tok_rows, width), bf16)] * 2,
        [
            pltpu.VMEM((tok_rows, width), f32),
            pltpu.VMEM((devices,) + w_out.shape, bf16),
            pltpu.VMEM((tok_rows, devices * tok_rows), f32),
            pltpu.VMEM((num_heads, tok_rows, HD), bf16),
            pltpu.VMEM((kv_heads, devices * tok_rows, HD), bf16),
            pltpu.VMEM((kv_heads, devices * tok_rows, HD), bf16),
            pltpu.VMEM((devices, tok_rows, w_out.shape[0]), bf16),
        ]
        + gather_sems(3, chips),
        1,
        raw_query, kv_all, cosine_pair, sine_pair, sinks, start, w_out, tokens, moe_gain[None, :],
        smem=(4,),
    )
    expert = me // 2
    slot_all = lax.dynamic_index_in_dim(meta_all, expert, 1, keepdims=False)
    weight_all = lax.dynamic_index_in_dim(meta_all, experts + expert, 1, keepdims=False)
    places = jnp.arange(padded, dtype=jnp.int32).astype(f32)
    select = (slot_all[:, None, :] == places[None, :, None]).astype(bf16)
    select_back = (slot_all[:, :, None] == places[None, None, :]).astype(bf16)
    partial = call(
        expert_kernel,
        chips,
        jax.ShapeDtypeStruct((devices, padded, width), bf16),
        [
            pltpu.VMEM((devices, tok_rows, width), bf16),
            pltpu.VMEM((4 * padded, width), bf16),
            pltpu.VMEM(w_gate.shape[1:], bf16),
            pltpu.VMEM(w_up.shape[1:], bf16),
            pltpu.VMEM(w_down.shape[:0:-1], bf16),
            pltpu.SemaphoreType.DMA((3,)),
        ]
        + gather_sems(2, chips),
        2,
        expert_in, select, w_gate[0], w_up[0], w_down[0].T,
        hbm=(2, 3, 4),
    )
    return call(
        combine_kernel,
        chips,
        jax.ShapeDtypeStruct((tok_rows, width), bf16),
        [pltpu.VMEM((chips, tok_rows, width), bf16)] * 2
        + [pltpu.VMEM((chips - 1, tok_rows, width), bf16)] * 2
        + ring_sems(2, chips),
        3,
        partial, select_back, weight_all[:, :, None], mixed,
    )


def solution(mesh):
    placed = (
        P(("groups", "ctx"), None),
        P("groups"),
        P(),
        P("ctx", None),
        P(),
        P(),
        P(),
        P("ctx", None),
        P(),
        P(("groups", "ctx"), None),
        P(("groups", "ctx"), None),
        P("ctx", None, None),
        P("ctx", None, None),
        P("ctx", None, None),
    )
    return jax.shard_map(
        per_device,
        mesh=mesh,
        in_specs=placed,
        out_specs=P(("groups", "ctx"), None),
        check_vma=False,
    )
```
